32 devices in a mesh: section: 4 (over x, core), blk: 8 (over z, y).
Axes of the slice: x: 2, y: 2, z: 4, core: 2. Of those that a mesh axis runs over, the one named last changes fastest.
Arguments:
- features: bfloat16 [4, 3072, 256], P(None, 'blk'), may hold values from -6 to 6
- pattern: int32 [4, 24, 3, 128, 128], P(None, 'blk'), may hold values 0 or 1
- col_block: int32 [4, 24, 3], P(None, 'blk'), may hold values from 0 to 23, as said below
- degree: int32 [4, 3072], P(None, 'blk'), may hold values from 4 to 24
- weight: bfloat16 [4, 256, 256], P('section'), may hold values from -0.375 to 0.375
- bias: float32 [4, 256], P('section'), may hold values from -3 to 3
Outputs:
- embeddings: bfloat16 [4, 3072, 256], P('section', 'blk')
The draws below stay inside these ranges and needn't reach their ends.
Inputs may be any that keep to these rules, and one draw needn't show every extreme that they name: col_block[c, b, k] lies within 1 block of b: slot 0 is b - 1 and slot 2 is b + 1, both clipped to the subgraph's blocks; the middle slots are anywhere in that range.
All inputs are finite; a program needn't handle non-finite values. No bound on the sum of `pattern` on one device may be relied on, other than what follows from the above.
Results may differ from the reference program's by a relative error of at most 0.012.
Values may be sent and summed in bfloat16 or wider, within the bound.
A program may use at most 64 MiB of HBM per device.

```python
import jax
import jax.numpy as jnp
from jax import lax

F = 256
TILE = 128
NT = 3
REACH = 1
NBLK = 24
NODES = 3072
LAYERS = 4
GROUPS = 4


def draw_col_block(key, part):
    block_ids = jnp.arange(NBLK, dtype=jnp.int32)[None, :, None]
    offsets = jax.random.randint(key, (GROUPS, NBLK, NT), -REACH, REACH + 1, dtype=jnp.int32)
    slot_ids = jnp.arange(NT, dtype=jnp.int32)[None, None, :]
    offsets = jnp.where(slot_ids == 0, -REACH, jnp.where(slot_ids == NT - 1, REACH, offsets))
    return jnp.clip(block_ids + offsets, 0, NBLK - 1).astype(jnp.int32)


def set_ends(entries, stream_key, low, top_value):
    shape = entries.shape
    place = [jax.random.randint(jax.random.fold_in(stream_key, axis), (), 0, shape[axis]) for axis in range(len(shape))]
    entries = entries.at[tuple(place)].set(low)
    longest = shape.index(max(shape))
    place[longest] = (place[longest] + 1) % shape[longest]
    return entries.at[tuple(place)].set(top_value)


def steps_of(key, extent, split, smallest, largest):
    loudness = 1.0
    for axis_at, shards_of in split:
        draws = jax.random.uniform(jax.random.fold_in(jax.random.fold_in(key, 6), axis_at), (shards_of,), jnp.float32, smallest / len(split), largest / len(split))
        loudness = loudness * jnp.repeat(jnp.exp(draws), extent[axis_at] // shards_of).reshape((-1,) + (1,) * (len(extent) - 1 - axis_at))
    return loudness


def scatter_about(key, dims, scale, limit, split=(), kind=jnp.bfloat16):
    array = scale * jax.random.normal(key, dims, jnp.float32)
    if split:
        array = array * steps_of(key, dims, split, -0.22, 0.18)
    return jnp.clip(array, -limit, limit).astype(kind)


def setup_inputs(seed: int = 0) -> dict:
    arg_keys = jax.random.split(jax.random.key(seed), 7)
    return {
        "features": scatter_about(arg_keys[0], (GROUPS, NODES, F), 1.0, 6.0, ((1, 8),)),
        "pattern": set_ends((jax.random.randint(arg_keys[1], (GROUPS, NBLK, NT, TILE, TILE), 0, 32) < 1).astype(jnp.int32), jax.random.fold_in(arg_keys[1], 1), 0, 1),
        "col_block": draw_col_block(jax.random.fold_in(arg_keys[6], 71), 0),
        "degree": set_ends(jax.random.randint(arg_keys[3], (GROUPS, NODES), 4, 25), jax.random.fold_in(arg_keys[3], 1), 4, 24).astype(jnp.int32),
        "weight": scatter_about(arg_keys[4], (LAYERS, F, F), F ** -0.5, 0.375, ((0, 4),)),
        "bias": scatter_about(arg_keys[5], (LAYERS, F), 0.5, 3.0, ((0, 4),), jnp.float32),
    }


def reference(features, pattern, col_block, degree, weight, bias):

    def one_group(group_args):
        start_rows, group_pattern, group_cols, group_degree = group_args
        inv_root = lax.rsqrt(group_degree.astype(jnp.float32))[:, None]
        tile_ones = group_pattern.astype(jnp.float32)

        def apply_layer(current, layer_params):
            layer_weight, layer_bias = layer_params
            scaled = (current.astype(jnp.float32) * inv_root).astype(jnp.bfloat16)
            own_blocks = scaled.reshape(NBLK, TILE, F)
            sources = jnp.take(own_blocks, group_cols, axis=0).astype(jnp.float32)
            summed = jnp.einsum('bkij,bkjf->bif', tile_ones, sources) + own_blocks.astype(jnp.float32)
            aggregate = (summed.reshape(NODES, F) * inv_root).astype(jnp.bfloat16)
            hidden = jnp.dot(aggregate, layer_weight, preferred_element_type=jnp.float32) + layer_bias
            updated = (current.astype(jnp.float32) + jax.nn.relu(hidden)).astype(jnp.bfloat16)
            return (updated, None)
        final_rows, unused = lax.scan(apply_layer, start_rows, (weight, bias))
        return final_rows
    return lax.map(one_group, (features, pattern, col_block, degree))
```

```python
import functools

import jax
import jax.numpy as jnp
from jax import lax
from jax.experimental import pallas as pl
from jax.experimental.pallas import tpu as pltpu
from jax.sharding import PartitionSpec as P

MESH = pl.DeviceIdType.MESH
REACH = 1
SPAN = 2 * REACH + 1


def kernel(
    sections, slabs, feat, pat, col, deg, w, b, out,
    xcur, pt, amat, own, low, high, wbuf, bbuf,
    load_sem, halo_send, halo_recv, w_send, w_recv, b_send, b_recv, f_send, fb_send,
):
    layers = wbuf.shape[0]
    per_dev, slots, tile = pt.shape[0], pt.shape[1], pt.shape[2]
    sec = lax.axis_index("section")
    slab = lax.axis_index("blk")
    partner = sec + 1 - 2 * (sec % 2)
    pairs = sections // 2
    others = [(sec + 2 * step) % sections for step in range(1, pairs)]

    loads = [
        pltpu.make_async_copy(feat.at[sec], xcur, load_sem.at[0]),
        pltpu.make_async_copy(pat.at[sec], pt, load_sem.at[1]),
        pltpu.make_async_copy(w.at[0], wbuf.at[sec], load_sem.at[2]),
        pltpu.make_async_copy(b, bbuf.at[sec], load_sem.at[3]),
    ]
    for load in loads:
        load.start()

    has_low = slab > 0
    has_high = slab < slabs - 1
    barrier = pltpu.get_barrier_semaphore()
    for peer in [partner] + others:
        pl.semaphore_signal(barrier, inc=1, device_id={"section": peer}, device_id_type=MESH)

    @pl.when(has_low)
    def _():
        pl.semaphore_signal(barrier, inc=1, device_id={"blk": slab - 1}, device_id_type=MESH)

    @pl.when(has_high)
    def _():
        pl.semaphore_signal(barrier, inc=1, device_id={"blk": slab + 1}, device_id_type=MESH)

    row_ids = lax.broadcasted_iota(jnp.int32, (tile, tile), 0)
    col_ids = lax.broadcasted_iota(jnp.int32, (tile, tile), 1)
    eye = jnp.where(row_ids == col_ids, 1.0, 0.0).astype(jnp.float32)

    def rows(i):
        return slice(i * tile, (i + 1) * tile)

    inv_row = lax.rsqrt(deg[pl.ds(sec, 1), :].astype(jnp.float32))
    inv = [jnp.sum(eye * inv_row[:, rows(i)], axis=1, keepdims=True) for i in range(per_dev)]

    loads[0].wait()
    for i in range(per_dev):
        own[0, rows(i), :] = (xcur[rows(i), :].astype(jnp.float32) * inv[i]).astype(jnp.bfloat16)

    @pl.when(jnp.logical_not(has_low))
    def _():
        low[...] = jnp.zeros_like(low)

    @pl.when(jnp.logical_not(has_high))
    def _():
        high[...] = jnp.zeros_like(high)

    pl.semaphore_wait(barrier, pairs + has_low.astype(jnp.int32) + has_high.astype(jnp.int32))

    def to_low(layer):
        return pltpu.make_async_remote_copy(
            src_ref=own.at[layer, rows(0), :], dst_ref=high.at[layer],
            send_sem=halo_send.at[layer, 0], recv_sem=halo_recv.at[layer, 1],
            device_id={"blk": slab - 1}, device_id_type=MESH,
        )

    def to_high(layer):
        return pltpu.make_async_remote_copy(
            src_ref=own.at[layer, rows(per_dev - 1), :], dst_ref=low.at[layer],
            send_sem=halo_send.at[layer, 1], recv_sem=halo_recv.at[layer, 0],
            device_id={"blk": slab + 1}, device_id_type=MESH,
        )

    def send_low(layer):
        @pl.when(has_low)
        def _():
            to_low(layer).start()

    def send_high(layer):
        @pl.when(has_high)
        def _():
            to_high(layer).start()

    def wait_low(layer):
        @pl.when(has_low)
        def _():
            to_high(layer).wait_recv()

    def wait_high(layer):
        @pl.when(has_high)
        def _():
            to_low(layer).wait_recv()

    def weight_copies(src_w, src_b, index, send_w, send_b, peer):
        return [
            pltpu.make_async_remote_copy(
                src_ref=src, dst_ref=buf.at[index], send_sem=ssem, recv_sem=rsem.at[index],
                device_id={"section": peer}, device_id_type=MESH,
            )
            for src, buf, ssem, rsem in (
                (src_w, wbuf, send_w, w_recv), (src_b, bbuf, send_b, b_recv),
            )
        ]

    send_low(0)
    send_high(0)
    own_sends = []
    for n, peer in enumerate(others + [partner]):
        own_sends += weight_copies(w.at[0], b, sec, w_send.at[n], b_send.at[n], peer)
    for copy in own_sends:
        copy.start()

    def forward(layer):
        return weight_copies(
            wbuf.at[layer], bbuf.at[layer], layer, f_send.at[layer], fb_send.at[layer], partner
        )

    passes_on = [
        jnp.logical_and(sec % 2 == layer % 2, sec != layer) for layer in range(layers)
    ]

    def take_weight(layer):
        @pl.when(sec != layer)
        def _():
            for copy in forward(layer):
                copy.wait_recv()

        @pl.when(passes_on[layer])
        def _():
            for copy in forward(layer):
                copy.start()

    loads[1].wait()
    for i in range(per_dev):
        merged = [jnp.zeros((tile, tile), jnp.float32) for _ in range(SPAN)]
        merged[REACH] = eye
        for slot in range(slots):
            ones = pt[i, slot].astype(jnp.float32)
            offset = col[i, sec, slot] - (slab * per_dev + i) + REACH
            for place in range(SPAN):
                merged[place] += ones * jnp.where(offset == place, 1.0, 0.0)
        for place in range(SPAN):
            amat[i, :, rows(place)] = merged[place].astype(jnp.bfloat16)
    loads[2].wait()
    loads[3].wait()

    def dot(x, y):
        return jnp.dot(x, y, preferred_element_type=jnp.float32)

    for layer in range(layers):
        def finish(i, summed):
            aggregate = (summed * inv[i]).astype(jnp.bfloat16)
            hidden = dot(aggregate, wbuf[layer]) + bbuf[layer]
            new = (xcur[rows(i), :].astype(jnp.float32) + jnp.maximum(hidden, 0.0)).astype(jnp.bfloat16)
            if layer == layers - 1:
                out[0, rows(i), :] = new
            else:
                xcur[rows(i), :] = new
                own[layer + 1, rows(i), :] = (new.astype(jnp.float32) * inv[i]).astype(jnp.bfloat16)

        last = per_dev - 1
        first_part = dot(amat[0, :, tile:], own[layer, : 2 * tile, :])
        last_part = dot(amat[last, :, : 2 * tile], own[layer, (last - 1) * tile :, :])
        inner = [dot(amat[i], own[layer, (i - 1) * tile : (i + 2) * tile, :]) for i in range(1, last)]
        take_weight(layer)
        for i in range(1, last):
            finish(i, inner[i - 1])
        wait_low(layer)
        finish(0, first_part + dot(amat[0, :, :tile], low[layer]))
        if layer < layers - 1:
            send_low(layer + 1)
        wait_high(layer)
        finish(last, last_part + dot(amat[last, :, 2 * tile :], high[layer]))
        if layer < layers - 1:
            send_high(layer + 1)

    for copy in own_sends:
        copy.wait_send()
    for layer in range(layers):
        @pl.when(has_low)
        def _():
            to_low(layer).wait_send()

        @pl.when(has_high)
        def _():
            to_high(layer).wait_send()

        @pl.when(passes_on[layer])
        def _():
            for copy in forward(layer):
                copy.wait_send()


def solution(mesh):
    sections, slabs = mesh.shape["section"], mesh.shape["blk"]

    def shards(features, pattern, col_block, degree, weight, bias):
        groups, slab_rows, width = features.shape
        per_dev, slots, tile = pattern.shape[1:4]
        layers = sections * weight.shape[0]
        assert groups == sections and weight.shape[0] == 1 and sections % 2 == 0 and per_dev >= 2
        bf16, f32 = jnp.bfloat16, jnp.float32
        dma = pltpu.SemaphoreType.DMA
        hbm = pl.BlockSpec(memory_space=pl.ANY)
        vmem = pl.BlockSpec(memory_space=pltpu.VMEM)
        peers = sections // 2
        return pl.pallas_call(
            functools.partial(kernel, sections, slabs),
            out_shape=jax.ShapeDtypeStruct((1, slab_rows, width), bf16),
            in_specs=[hbm, hbm, pl.BlockSpec(memory_space=pltpu.SMEM), vmem, hbm, hbm],
            out_specs=vmem,
            scratch_shapes=[
                pltpu.VMEM((slab_rows, width), bf16),
                pltpu.VMEM((per_dev, slots, tile, tile), jnp.int32),
                pltpu.VMEM((per_dev, tile, SPAN * tile), bf16),
                pltpu.VMEM((layers, slab_rows, width), bf16),
                pltpu.VMEM((layers, tile, width), bf16),
                pltpu.VMEM((layers, tile, width), bf16),
                pltpu.VMEM((layers, width, width), bf16),
                pltpu.VMEM((layers, 1, width), f32),
                dma((4,)),
                dma((layers, 2)),
                dma((layers, 2)),
                dma((peers,)),
                dma((layers,)),
                dma((peers,)),
                dma((layers,)),
                dma((layers,)),
                dma((layers,)),
            ],
            compiler_params=pltpu.CompilerParams(collective_id=0, has_side_effects=True),
        )(features, pattern, jnp.transpose(col_block, (1, 0, 2)), degree, weight, bias)

    return jax.shard_map(
        shards,
        mesh=mesh,
        in_specs=(
            P(None, "blk", None),
            P(None, "blk", None, None, None),
            P(None, "blk", None),
            P(None, "blk"),
            P("section", None, None),
            P("section", None),
        ),
        out_specs=P("section", "blk", None),
        check_vma=False,
    )
```

```python
import functools

import jax
import jax.numpy as jnp
from jax import lax
from jax.experimental import pallas as pl
from jax.experimental.pallas import tpu as pltpu
from jax.sharding import PartitionSpec as P

MESH = pl.DeviceIdType.MESH
REACH = 1
SPAN = 2 * REACH + 1


def kernel(
    sections, slabs, feat, pat, col, deg, w, b, out,
    xcur, pt, inv, edge_halo, edge_own, inner_adj, own, halo, wbuf, bbuf,
    load_sem, halo_send, halo_recv, w_send, w_recv, b_send, b_recv, f_send, fb_send,
):
    layers = wbuf.shape[0]
    per_dev, slots, tile = pt.shape[0], pt.shape[1], pt.shape[2]
    sec = lax.axis_index("section")
    slab = lax.axis_index("blk")
    partner = sec + 1 - 2 * (sec % 2)
    pairs = sections // 2
    others = [(sec + 2 * step) % sections for step in range(1, pairs)]

    loads = [
        pltpu.make_async_copy(feat.at[sec], xcur, load_sem.at[0]),
        pltpu.make_async_copy(pat.at[sec], pt, load_sem.at[1]),
        pltpu.make_async_copy(w.at[0], wbuf.at[sec], load_sem.at[2]),
        pltpu.make_async_copy(b, bbuf.at[sec], load_sem.at[3]),
    ]
    for load in loads:
        load.start()

    far, near = slab % 2, 1 - slab % 2

    def peer_of(side):
        return slab + 2 * side - 1

    def has(side):
        return jnp.logical_and(peer_of(side) >= 0, peer_of(side) < slabs)

    barrier = pltpu.get_barrier_semaphore()
    for peer in [partner] + others:
        pl.semaphore_signal(barrier, inc=1, device_id={"section": peer}, device_id_type=MESH)

    for side in (far, near):
        @pl.when(has(side))
        def _():
            pl.semaphore_signal(
                barrier, inc=1, device_id={"blk": peer_of(side)}, device_id_type=MESH
            )

    row_ids = lax.broadcasted_iota(jnp.int32, (tile, tile), 0)
    col_ids = lax.broadcasted_iota(jnp.int32, (tile, tile), 1)
    eye = jnp.where(row_ids == col_ids, 1.0, 0.0).astype(jnp.float32)

    def rows(i):
        return slice(i * tile, (i + 1) * tile)

    inv_row = lax.rsqrt(deg[pl.ds(sec, 1), :].astype(jnp.float32))
    for i in range(per_dev):
        column = jnp.sum(eye * inv_row[:, rows(i)], axis=1, keepdims=True)
        inv[rows(i), :] = jnp.broadcast_to(column, (tile, inv.shape[1]))

    loads[0].wait()
    own[0] = (xcur[...].astype(jnp.float32) * inv[...]).astype(jnp.bfloat16)

    for side in (far, near):
        @pl.when(jnp.logical_not(has(side)))
        def _():
            for layer in range(layers):
                halo[layer, side] = jnp.zeros(halo.shape[2:], halo.dtype)

    pl.semaphore_wait(
        barrier, pairs + has(far).astype(jnp.int32) + has(near).astype(jnp.int32)
    )

    last = per_dev - 1

    def edge_rows(side):
        return pl.ds(pl.multiple_of(side * last * tile, tile), tile)

    def edge_pair(side):
        return pl.ds(pl.multiple_of(side * (last - 1) * tile, tile), 2 * tile)

    def halo_copy(layer, side):
        return pltpu.make_async_remote_copy(
            src_ref=own.at[layer, edge_rows(side), :], dst_ref=halo.at[layer, 1 - side],
            send_sem=halo_send.at[layer, side], recv_sem=halo_recv.at[layer, 1 - side],
            device_id={"blk": peer_of(side)}, device_id_type=MESH,
        )

    def arrival(layer, side):
        return pltpu.make_async_remote_copy(
            src_ref=own.at[layer, edge_rows(side), :], dst_ref=halo.at[layer, side],
            send_sem=halo_send.at[layer, side], recv_sem=halo_recv.at[layer, side],
            device_id={"blk": peer_of(side)}, device_id_type=MESH,
        )

    def send(layer, side):
        @pl.when(has(side))
        def _():
            halo_copy(layer, side).start()

    def take(layer, side):
        @pl.when(has(side))
        def _():
            arrival(layer, side).wait_recv()

    def sent(layer, side):
        @pl.when(has(side))
        def _():
            halo_copy(layer, side).wait_send()

    def weight_copies(src_w, src_b, index, send_w, send_b, peer):
        return [
            pltpu.make_async_remote_copy(
                src_ref=src, dst_ref=buf.at[index], send_sem=ssem, recv_sem=rsem.at[index],
                device_id={"section": peer}, device_id_type=MESH,
            )
            for src, buf, ssem, rsem in (
                (src_w, wbuf, send_w, w_recv), (src_b, bbuf, send_b, b_recv),
            )
        ]

    send(0, far)
    send(0, near)
    own_sends = []
    for n, peer in enumerate(others + [partner]):
        own_sends += weight_copies(w.at[0], b, sec, w_send.at[n], b_send.at[n], peer)
    for copy in own_sends:
        copy.start()

    def forward(layer):
        return weight_copies(
            wbuf.at[layer], bbuf.at[layer], layer, f_send.at[layer], fb_send.at[layer], partner
        )

    passes_on = [
        jnp.logical_and(sec % 2 == layer % 2, sec != layer) for layer in range(layers)
    ]

    def take_weight(layer):
        @pl.when(sec != layer)
        def _():
            for copy in forward(layer):
                copy.wait_recv()

        @pl.when(passes_on[layer])
        def _():
            for copy in forward(layer):
                copy.start()

    loads[1].wait()
    for i in range(per_dev):
        merged = [jnp.zeros((tile, tile), jnp.float32) for _ in range(SPAN)]
        merged[REACH] = eye
        for slot in range(slots):
            ones = pt[i, slot].astype(jnp.float32)
            offset = col[i, sec, slot] - (slab * per_dev + i) + REACH
            for place in range(SPAN):
                merged[place] += ones * jnp.where(offset == place, 1.0, 0.0)
        merged = [part.astype(jnp.bfloat16) for part in merged]
        if i == 0:
            edge_halo[0] = merged[0]
            edge_own[0, :, :tile] = merged[1]
            edge_own[0, :, tile:] = merged[2]
        elif i == last:
            edge_own[1, :, :tile] = merged[0]
            edge_own[1, :, tile:] = merged[1]
            edge_halo[1] = merged[2]
        else:
            for place in range(SPAN):
                inner_adj[i - 1, :, rows(place)] = merged[place]
    loads[2].wait()
    loads[3].wait()

    def dot(x, y):
        return jnp.dot(x, y, preferred_element_type=jnp.float32)

    def finish(layer, place, summed):
        scale = inv[place, :]
        aggregate = (summed * scale).astype(jnp.bfloat16)
        hidden = dot(aggregate, wbuf[layer]) + bbuf[layer]
        new = xcur[place, :].astype(jnp.float32) + jnp.maximum(hidden, 0.0)
        new = new.astype(jnp.bfloat16)
        if layer == layers - 1:
            out[0, place, :] = new
        else:
            xcur[place, :] = new
            own[layer + 1, place, :] = (new.astype(jnp.float32) * scale).astype(jnp.bfloat16)

    def edge_part(layer, side):
        return dot(edge_own[side], own[layer, edge_pair(side), :])

    far_part, near_part = edge_part(0, far), edge_part(0, near)
    take_weight(0)
    for layer in range(layers):
        more = layer < layers - 1
        take(layer, far)
        finish(layer, edge_rows(far), far_part + dot(edge_halo[far], halo[layer, far]))
        if more:
            send(layer + 1, far)
        take(layer, near)
        finish(layer, edge_rows(near), near_part + dot(edge_halo[near], halo[layer, near]))
        if more:
            send(layer + 1, near)
        for i in range(1, last):
            inner = dot(inner_adj[i - 1], own[layer, (i - 1) * tile : (i + 2) * tile, :])
            finish(layer, rows(i), inner)
        if more:
            far_part, near_part = edge_part(layer + 1, far), edge_part(layer + 1, near)
            take_weight(layer + 1)

    for copy in own_sends:
        copy.wait_send()
    for layer in range(layers):
        sent(layer, far)
        sent(layer, near)

        @pl.when(passes_on[layer])
        def _():
            for copy in forward(layer):
                copy.wait_send()


def solution(mesh):
    sections, slabs = mesh.shape["section"], mesh.shape["blk"]

    def shards(features, pattern, col_block, degree, weight, bias):
        groups, slab_rows, width = features.shape
        per_dev, slots, tile = pattern.shape[1:4]
        layers = sections * weight.shape[0]
        assert groups == sections and weight.shape[0] == 1 and sections % 2 == 0 and per_dev >= 2
        bf16, f32 = jnp.bfloat16, jnp.float32
        dma = pltpu.SemaphoreType.DMA
        hbm = pl.BlockSpec(memory_space=pl.ANY)
        vmem = pl.BlockSpec(memory_space=pltpu.VMEM)
        peers = sections // 2
        return pl.pallas_call(
            functools.partial(kernel, sections, slabs),
            out_shape=pltpu.VMEM((1, slab_rows, width), bf16),
            in_specs=[hbm, hbm, pl.BlockSpec(memory_space=pltpu.SMEM), vmem, hbm, hbm],
            out_specs=vmem,
            scratch_shapes=[
                pltpu.VMEM((slab_rows, width), bf16),
                pltpu.VMEM((per_dev, slots, tile, tile), jnp.int32),
                pltpu.VMEM((slab_rows, width), f32),
                pltpu.VMEM((2, tile, tile), bf16),
                pltpu.VMEM((2, tile, 2 * tile), bf16),
                pltpu.VMEM((max(per_dev - 2, 1), tile, SPAN * tile), bf16),
                pltpu.VMEM((layers, slab_rows, width), bf16),
                pltpu.VMEM((layers, 2, tile, width), bf16),
                pltpu.VMEM((layers, width, width), bf16),
                pltpu.VMEM((layers, 1, width), f32),
                dma((4,)),
                dma((layers, 2)),
                dma((layers, 2)),
                dma((peers,)),
                dma((layers,)),
                dma((peers,)),
                dma((layers,)),
                dma((layers,)),
                dma((layers,)),
            ],
            compiler_params=pltpu.CompilerParams(collective_id=0, has_side_effects=True),
        )(features, pattern, jnp.transpose(col_block, (1, 0, 2)), degree, weight, bias)

    return jax.shard_map(
        shards,
        mesh=mesh,
        in_specs=(
            P(None, "blk", None),
            P(None, "blk", None, None, None),
            P(None, "blk", None),
            P(None, "blk"),
            P("section", None, None),
            P("section", None),
        ),
        out_specs=P("section", "blk", None),
        check_vma=False,
    )
```

```python
import functools

import jax
import jax.numpy as jnp
from jax import lax
from jax.experimental import pallas as pl
from jax.experimental.pallas import tpu as pltpu
from jax.sharding import PartitionSpec as P

MESH = pl.DeviceIdType.MESH
REACH = 1
SPAN = 2 * REACH + 1


def kernel(
    sections, slabs, feat, pat, col_hbm, deg_hbm, w, b, out,
    col, deg, xcur, pt, inv, edge_halo, edge_own, inner_adj, own, halo, wbuf, bbuf,
    load_sem, halo_send, halo_recv, w_send, w_recv, b_send, b_recv, f_send, fb_send,
):
    layers = wbuf.shape[0]
    per_dev, slots, tile = pt.shape[0], pt.shape[1], pt.shape[2]
    sec = lax.axis_index("section")
    slab = lax.axis_index("blk")
    partner = sec + 1 - 2 * (sec % 2)
    pairs = sections // 2
    others = [(sec + 2 * step) % sections for step in range(1, pairs)]

    col_load = pltpu.make_async_copy(col_hbm, col, load_sem.at[5])
    col_load.start()
    deg_load = pltpu.make_async_copy(deg_hbm, deg, load_sem.at[4])
    deg_load.start()
    loads = [
        pltpu.make_async_copy(feat.at[sec], xcur, load_sem.at[0]),
        pltpu.make_async_copy(pat.at[sec], pt, load_sem.at[1]),
        pltpu.make_async_copy(w.at[0], wbuf.at[sec], load_sem.at[2]),
        pltpu.make_async_copy(b, bbuf.at[sec], load_sem.at[3]),
    ]
    for load in loads:
        load.start()

    far, near = slab % 2, 1 - slab % 2

    def peer_of(side):
        return slab + 2 * side - 1

    def has(side):
        return jnp.logical_and(peer_of(side) >= 0, peer_of(side) < slabs)

    barrier = pltpu.get_barrier_semaphore()
    for peer in [partner] + others:
        pl.semaphore_signal(barrier, inc=1, device_id={"section": peer}, device_id_type=MESH)

    for side in (far, near):
        @pl.when(has(side))
        def _():
            pl.semaphore_signal(
                barrier, inc=1, device_id={"blk": peer_of(side)}, device_id_type=MESH
            )

    row_ids = lax.broadcasted_iota(jnp.int32, (tile, tile), 0)
    col_ids = lax.broadcasted_iota(jnp.int32, (tile, tile), 1)
    eye = jnp.where(row_ids == col_ids, 1.0, 0.0).astype(jnp.float32)

    def rows(i):
        return slice(i * tile, (i + 1) * tile)

    deg_load.wait()
    inv_row = lax.rsqrt(deg[pl.ds(sec, 1), :].astype(jnp.float32))
    for i in range(per_dev):
        column = jnp.sum(eye * inv_row[:, rows(i)], axis=1, keepdims=True)
        inv[rows(i), :] = jnp.broadcast_to(column, (tile, inv.shape[1]))

    loads[0].wait()
    own[0] = (xcur[...].astype(jnp.float32) * inv[...]).astype(jnp.bfloat16)

    for side in (far, near):
        @pl.when(jnp.logical_not(has(side)))
        def _():
            for layer in range(layers):
                halo[layer, side] = jnp.zeros(halo.shape[2:], halo.dtype)

    pl.semaphore_wait(
        barrier, pairs + has(far).astype(jnp.int32) + has(near).astype(jnp.int32)
    )

    last = per_dev - 1

    def edge_rows(side):
        return pl.ds(pl.multiple_of(side * last * tile, tile), tile)

    def edge_pair(side):
        return pl.ds(pl.multiple_of(side * (last - 1) * tile, tile), 2 * tile)

    def halo_copy(layer, side):
        return pltpu.make_async_remote_copy(
            src_ref=own.at[layer, edge_rows(side), :], dst_ref=halo.at[layer, 1 - side],
            send_sem=halo_send.at[layer, side], recv_sem=halo_recv.at[layer, 1 - side],
            device_id={"blk": peer_of(side)}, device_id_type=MESH,
        )

    def arrival(layer, side):
        return pltpu.make_async_remote_copy(
            src_ref=own.at[layer, edge_rows(side), :], dst_ref=halo.at[layer, side],
            send_sem=halo_send.at[layer, side], recv_sem=halo_recv.at[layer, side],
            device_id={"blk": peer_of(side)}, device_id_type=MESH,
        )

    def send(layer, side):
        @pl.when(has(side))
        def _():
            halo_copy(layer, side).start()

    def take(layer, side):
        @pl.when(has(side))
        def _():
            arrival(layer, side).wait_recv()

    def sent(layer, side):
        @pl.when(has(side))
        def _():
            halo_copy(layer, side).wait_send()

    def weight_copies(src_w, src_b, index, send_w, send_b, peer):
        return [
            pltpu.make_async_remote_copy(
                src_ref=src, dst_ref=buf.at[index], send_sem=ssem, recv_sem=rsem.at[index],
                device_id={"section": peer}, device_id_type=MESH,
            )
            for src, buf, ssem, rsem in (
                (src_w, wbuf, send_w, w_recv), (src_b, bbuf, send_b, b_recv),
            )
        ]

    send(0, far)
    send(0, near)
    own_sends = []
    for n, peer in enumerate(others + [partner]):
        own_sends += weight_copies(w.at[0], b, sec, w_send.at[n], b_send.at[n], peer)
    for copy in own_sends:
        copy.start()

    def forward(layer):
        return weight_copies(
            wbuf.at[layer], bbuf.at[layer], layer, f_send.at[layer], fb_send.at[layer], partner
        )

    passes_on = [
        jnp.logical_and(sec % 2 == layer % 2, sec != layer) for layer in range(layers)
    ]

    def take_weight(layer):
        @pl.when(sec != layer)
        def _():
            for copy in forward(layer):
                copy.wait_recv()

        @pl.when(passes_on[layer])
        def _():
            for copy in forward(layer):
                copy.start()

    loads[1].wait()
    col_load.wait()
    for i in range(per_dev):
        merged = [jnp.zeros((tile, tile), jnp.float32) for _ in range(SPAN)]
        merged[REACH] = eye
        for slot in range(slots):
            ones = pt[i, slot].astype(jnp.float32)
            offset = col[i, sec, slot] - (slab * per_dev + i) + REACH
            for place in range(SPAN):
                merged[place] += ones * jnp.where(offset == place, 1.0, 0.0)
        merged = [part.astype(jnp.bfloat16) for part in merged]
        if i == 0:
            edge_halo[0] = merged[0]
            edge_own[0, :, :tile] = merged[1]
            edge_own[0, :, tile:] = merged[2]
        elif i == last:
            edge_own[1, :, :tile] = merged[0]
            edge_own[1, :, tile:] = merged[1]
            edge_halo[1] = merged[2]
        else:
            for place in range(SPAN):
                inner_adj[i - 1, :, rows(place)] = merged[place]
    loads[2].wait()
    loads[3].wait()

    def dot(x, y):
        return jnp.dot(x, y, preferred_element_type=jnp.float32)

    def finish(layer, place, summed):
        scale = inv[place, :]
        aggregate = (summed * scale).astype(jnp.bfloat16)
        hidden = dot(aggregate, wbuf[layer]) + bbuf[layer]
        new = xcur[place, :].astype(jnp.float32) + jnp.maximum(hidden, 0.0)
        new = new.astype(jnp.bfloat16)
        if layer == layers - 1:
            out[0, place, :] = new
        else:
            xcur[place, :] = new
            own[layer + 1, place, :] = (new.astype(jnp.float32) * scale).astype(jnp.bfloat16)

    def edge_part(layer, side):
        return dot(edge_own[side], own[layer, edge_pair(side), :])

    far_part, near_part = edge_part(0, far), edge_part(0, near)
    take_weight(0)
    for layer in range(layers):
        more = layer < layers - 1
        take(layer, far)
        finish(layer, edge_rows(far), far_part + dot(edge_halo[far], halo[layer, far]))
        if more:
            send(layer + 1, far)
        take(layer, near)
        finish(layer, edge_rows(near), near_part + dot(edge_halo[near], halo[layer, near]))
        if more:
            send(layer + 1, near)
        for i in range(1, last):
            inner = dot(inner_adj[i - 1], own[layer, (i - 1) * tile : (i + 2) * tile, :])
            finish(layer, rows(i), inner)
        if more:
            far_part, near_part = edge_part(layer + 1, far), edge_part(layer + 1, near)
            take_weight(layer + 1)

    for copy in own_sends:
        copy.wait_send()
    for layer in range(layers):
        sent(layer, far)
        sent(layer, near)

        @pl.when(passes_on[layer])
        def _():
            for copy in forward(layer):
                copy.wait_send()


def solution(mesh):
    sections, slabs = mesh.shape["section"], mesh.shape["blk"]

    def shards(features, pattern, col_block, degree, weight, bias):
        groups, slab_rows, width = features.shape
        per_dev, slots, tile = pattern.shape[1:4]
        layers = sections * weight.shape[0]
        assert groups == sections and weight.shape[0] == 1 and sections % 2 == 0 and per_dev >= 2
        bf16, f32 = jnp.bfloat16, jnp.float32
        dma = pltpu.SemaphoreType.DMA
        hbm = pl.BlockSpec(memory_space=pl.ANY)
        vmem = pl.BlockSpec(memory_space=pltpu.VMEM)
        peers = sections // 2
        return pl.pallas_call(
            functools.partial(kernel, sections, slabs),
            out_shape=pltpu.VMEM((1, slab_rows, width), bf16),
            in_specs=[hbm, hbm, hbm, hbm, hbm, hbm],
            out_specs=vmem,
            scratch_shapes=[
                pltpu.SMEM((per_dev, groups, slots), jnp.int32),
                pltpu.VMEM(degree.shape, jnp.int32),
                pltpu.VMEM((slab_rows, width), bf16),
                pltpu.VMEM((per_dev, slots, tile, tile), jnp.int32),
                pltpu.VMEM((slab_rows, width), f32),
                pltpu.VMEM((2, tile, tile), bf16),
                pltpu.VMEM((2, tile, 2 * tile), bf16),
                pltpu.VMEM((max(per_dev - 2, 1), tile, SPAN * tile), bf16),
                pltpu.VMEM((layers, slab_rows, width), bf16),
                pltpu.VMEM((layers, 2, tile, width), bf16),
                pltpu.VMEM((layers, width, width), bf16),
                pltpu.VMEM((layers, 1, width), f32),
                dma((6,)),
                dma((layers, 2)),
                dma((layers, 2)),
                dma((peers,)),
                dma((layers,)),
                dma((peers,)),
                dma((layers,)),
                dma((layers,)),
                dma((layers,)),
            ],
            compiler_params=pltpu.CompilerParams(collective_id=0, has_side_effects=True),
        )(features, pattern, jnp.transpose(col_block, (1, 0, 2)), degree, weight, bias)

    return jax.shard_map(
        shards,
        mesh=mesh,
        in_specs=(
            P(None, "blk", None),
            P(None, "blk", None, None, None),
            P(None, "blk", None),
            P(None, "blk"),
            P("section", None, None),
            P("section", None),
        ),
        out_specs=P("section", "blk", None),
        check_vma=False,
    )
```

```python
import functools

import jax
import jax.numpy as jnp
from jax import lax
from jax.experimental import pallas as pl
from jax.experimental.pallas import tpu as pltpu
from jax.sharding import PartitionSpec as P

MESH = pl.DeviceIdType.MESH
REACH = 1
SPAN = 2 * REACH + 1


def kernel(
    sections, slabs, feat, pat, col_hbm, deg_hbm, w, b, out,
    col, deg, xcur, pt, inv, edge_halo, edge_own, inner_adj, own, halo, wbuf, bbuf,
    load_sem, halo_send, halo_recv, w_send, w_recv, b_send, b_recv, f_send, fb_send,
):
    layers = wbuf.shape[0]
    per_dev, slots, tile = pt.shape[0], pt.shape[1], pt.shape[2]
    sec = lax.axis_index("section")
    slab = lax.axis_index("blk")
    partner = sec + 1 - 2 * (sec % 2)
    pairs = sections // 2
    others = [(sec + 2 * step) % sections for step in range(1, pairs)]

    far, near = slab % 2, 1 - slab % 2

    def peer_of(side):
        return slab + 2 * side - 1

    def has(side):
        return jnp.logical_and(peer_of(side) >= 0, peer_of(side) < slabs)

    barrier = pltpu.get_barrier_semaphore()
    for peer in [partner] + others:
        pl.semaphore_signal(barrier, inc=1, device_id={"section": peer}, device_id_type=MESH)

    for side in (far, near):
        @pl.when(has(side))
        def _():
            pl.semaphore_signal(
                barrier, inc=1, device_id={"blk": peer_of(side)}, device_id_type=MESH
            )

    col_load = pltpu.make_async_copy(col_hbm, col, load_sem.at[5])
    col_load.start()
    deg_load = pltpu.make_async_copy(deg_hbm, deg, load_sem.at[4])
    deg_load.start()
    loads = [
        pltpu.make_async_copy(feat.at[sec], xcur, load_sem.at[0]),
        pltpu.make_async_copy(pat.at[sec], pt, load_sem.at[1]),
        pltpu.make_async_copy(w.at[0], wbuf.at[sec], load_sem.at[2]),
        pltpu.make_async_copy(b, bbuf.at[sec], load_sem.at[3]),
    ]
    for load in loads:
        load.start()

    row_ids = lax.broadcasted_iota(jnp.int32, (tile, tile), 0)
    col_ids = lax.broadcasted_iota(jnp.int32, (tile, tile), 1)
    eye = jnp.where(row_ids == col_ids, 1.0, 0.0).astype(jnp.float32)

    def rows(i):
        return slice(i * tile, (i + 1) * tile)

    deg_load.wait()
    inv_row = lax.rsqrt(deg[pl.ds(sec, 1), :].astype(jnp.float32))
    for i in range(per_dev):
        column = jnp.sum(eye * inv_row[:, rows(i)], axis=1, keepdims=True)
        inv[rows(i), :] = jnp.broadcast_to(column, (tile, inv.shape[1]))

    loads[0].wait()
    for i in (0, per_dev - 1):
        own[0, rows(i), :] = (xcur[rows(i), :].astype(jnp.float32) * inv[rows(i), :]).astype(jnp.bfloat16)

    for side in (far, near):
        @pl.when(jnp.logical_not(has(side)))
        def _():
            for layer in range(layers):
                halo[layer, side] = jnp.zeros(halo.shape[2:], halo.dtype)

    pl.semaphore_wait(
        barrier, pairs + has(far).astype(jnp.int32) + has(near).astype(jnp.int32)
    )

    last = per_dev - 1

    def edge_rows(side):
        return pl.ds(pl.multiple_of(side * last * tile, tile), tile)

    def edge_pair(side):
        return pl.ds(pl.multiple_of(side * (last - 1) * tile, tile), 2 * tile)

    def halo_copy(layer, side):
        return pltpu.make_async_remote_copy(
            src_ref=own.at[layer, edge_rows(side), :], dst_ref=halo.at[layer, 1 - side],
            send_sem=halo_send.at[layer, side], recv_sem=halo_recv.at[layer, 1 - side],
            device_id={"blk": peer_of(side)}, device_id_type=MESH,
        )

    def arrival(layer, side):
        return pltpu.make_async_remote_copy(
            src_ref=own.at[layer, edge_rows(side), :], dst_ref=halo.at[layer, side],
            send_sem=halo_send.at[layer, side], recv_sem=halo_recv.at[layer, side],
            device_id={"blk": peer_of(side)}, device_id_type=MESH,
        )

    def send(layer, side):
        @pl.when(has(side))
        def _():
            halo_copy(layer, side).start()

    def take(layer, side):
        @pl.when(has(side))
        def _():
            arrival(layer, side).wait_recv()

    def sent(layer, side):
        @pl.when(has(side))
        def _():
            halo_copy(layer, side).wait_send()

    def weight_copies(src_w, src_b, index, send_w, send_b, peer):
        return [
            pltpu.make_async_remote_copy(
                src_ref=src, dst_ref=buf.at[index], send_sem=ssem, recv_sem=rsem.at[index],
                device_id={"section": peer}, device_id_type=MESH,
            )
            for src, buf, ssem, rsem in (
                (src_w, wbuf, send_w, w_recv), (src_b, bbuf, send_b, b_recv),
            )
        ]

    send(0, far)
    send(0, near)
    for i in range(1, last):
        own[0, rows(i), :] = (xcur[rows(i), :].astype(jnp.float32) * inv[rows(i), :]).astype(jnp.bfloat16)
    own_sends = []
    for n, peer in enumerate(others + [partner]):
        own_sends += weight_copies(w.at[0], b, sec, w_send.at[n], b_send.at[n], peer)
    for copy in own_sends:
        copy.start()

    def forward(layer):
        return weight_copies(
            wbuf.at[layer], bbuf.at[layer], layer, f_send.at[layer], fb_send.at[layer], partner
        )

    passes_on = [
        jnp.logical_and(sec % 2 == layer % 2, sec != layer) for layer in range(layers)
    ]

    def take_weight(layer):
        @pl.when(sec != layer)
        def _():
            for copy in forward(layer):
                copy.wait_recv()

        @pl.when(passes_on[layer])
        def _():
            for copy in forward(layer):
                copy.start()

    loads[1].wait()
    col_load.wait()
    for i in range(per_dev):
        merged = [jnp.zeros((tile, tile), jnp.float32) for _ in range(SPAN)]
        merged[REACH] = eye
        for slot in range(slots):
            ones = pt[i, slot].astype(jnp.float32)
            offset = col[i, sec, slot] - (slab * per_dev + i) + REACH
            for place in range(SPAN):
                merged[place] += ones * jnp.where(offset == place, 1.0, 0.0)
        merged = [part.astype(jnp.bfloat16) for part in merged]
        if i == 0:
            edge_halo[0] = merged[0]
            edge_own[0, :, :tile] = merged[1]
            edge_own[0, :, tile:] = merged[2]
        elif i == last:
            edge_own[1, :, :tile] = merged[0]
            edge_own[1, :, tile:] = merged[1]
            edge_halo[1] = merged[2]
        else:
            for place in range(SPAN):
                inner_adj[i - 1, :, rows(place)] = merged[place]
    loads[2].wait()
    loads[3].wait()

    def dot(x, y):
        return jnp.dot(x, y, preferred_element_type=jnp.float32)

    def finish(layer, place, summed):
        scale = inv[place, :]
        aggregate = (summed * scale).astype(jnp.bfloat16)
        hidden = dot(aggregate, wbuf[layer]) + bbuf[layer]
        new = xcur[place, :].astype(jnp.float32) + jnp.maximum(hidden, 0.0)
        new = new.astype(jnp.bfloat16)
        if layer == layers - 1:
            out[0, place, :] = new
        else:
            xcur[place, :] = new
            own[layer + 1, place, :] = (new.astype(jnp.float32) * scale).astype(jnp.bfloat16)

    def inner_rows(layer):
        for i in range(1, last):
            inner = dot(inner_adj[i - 1], own[layer, (i - 1) * tile : (i + 2) * tile, :])
            finish(layer, rows(i), inner)

    def edge_part(layer, side):
        return dot(edge_own[side], own[layer, edge_pair(side), :])

    far_part, near_part = edge_part(0, far), edge_part(0, near)
    take_weight(0)
    for layer in range(layers):
        more = layer < layers - 1
        if not more:
            inner_rows(layer)
        take(layer, far)
        finish(layer, edge_rows(far), far_part + dot(edge_halo[far], halo[layer, far]))
        if more:
            send(layer + 1, far)
        take(layer, near)
        finish(layer, edge_rows(near), near_part + dot(edge_halo[near], halo[layer, near]))
        if more:
            send(layer + 1, near)
        if more:
            inner_rows(layer)
        if more:
            far_part, near_part = edge_part(layer + 1, far), edge_part(layer + 1, near)
            take_weight(layer + 1)

    for copy in own_sends:
        copy.wait_send()
    for layer in range(layers):
        sent(layer, far)
        sent(layer, near)

        @pl.when(passes_on[layer])
        def _():
            for copy in forward(layer):
                copy.wait_send()


def solution(mesh):
    sections, slabs = mesh.shape["section"], mesh.shape["blk"]

    def shards(features, pattern, col_block, degree, weight, bias):
        groups, slab_rows, width = features.shape
        per_dev, slots, tile = pattern.shape[1:4]
        layers = sections * weight.shape[0]
        assert groups == sections and weight.shape[0] == 1 and sections % 2 == 0 and per_dev >= 2
        bf16, f32 = jnp.bfloat16, jnp.float32
        dma = pltpu.SemaphoreType.DMA
        hbm = pl.BlockSpec(memory_space=pl.ANY)
        vmem = pl.BlockSpec(memory_space=pltpu.VMEM)
        peers = sections // 2
        return pl.pallas_call(
            functools.partial(kernel, sections, slabs),
            out_shape=pltpu.VMEM((1, slab_rows, width), bf16),
            in_specs=[hbm, hbm, hbm, hbm, hbm, hbm],
            out_specs=vmem,
            scratch_shapes=[
                pltpu.SMEM((per_dev, groups, slots), jnp.int32),
                pltpu.VMEM(degree.shape, jnp.int32),
                pltpu.VMEM((slab_rows, width), bf16),
                pltpu.VMEM((per_dev, slots, tile, tile), jnp.int32),
                pltpu.VMEM((slab_rows, width), f32),
                pltpu.VMEM((2, tile, tile), bf16),
                pltpu.VMEM((2, tile, 2 * tile), bf16),
                pltpu.VMEM((max(per_dev - 2, 1), tile, SPAN * tile), bf16),
                pltpu.VMEM((layers, slab_rows, width), bf16),
                pltpu.VMEM((layers, 2, tile, width), bf16),
                pltpu.VMEM((layers, width, width), bf16),
                pltpu.VMEM((layers, 1, width), f32),
                dma((6,)),
                dma((layers, 2)),
                dma((layers, 2)),
                dma((peers,)),
                dma((layers,)),
                dma((peers,)),
                dma((layers,)),
                dma((layers,)),
                dma((layers,)),
            ],
            compiler_params=pltpu.CompilerParams(collective_id=0, has_side_effects=True),
        )(features, pattern, jnp.transpose(col_block, (1, 0, 2)), degree, weight, bias)

    return jax.shard_map(
        shards,
        mesh=mesh,
        in_specs=(
            P(None, "blk", None),
            P(None, "blk", None, None, None),
            P(None, "blk", None),
            P(None, "blk"),
            P("section", None, None),
            P("section", None),
        ),
        out_specs=P("section", "blk", None),
        check_vma=False,
    )
```
